32 devices in a mesh: row: 8 (over z, y), col: 4 (over x, core).
Axes of the slice: x: 2, y: 2, z: 4, core: 2. Of those that a mesh axis runs over, the one named last changes fastest.
Arguments:
- load_currents: float32 [32, 1024, 512], P(None, 'row', 'col'), may hold values from -36 to 36
- labels: int32 [1024, 512], P('row', 'col'), may hold values from 0 to 255, as said below
- bump_height: float32 [1024, 512], P('row', 'col'), may hold values from 0.5 to 2
- horizontal_class: int32 [1024, 512], P('row', 'col'), may hold values from 0 to 7
- vertical_class: int32 [1024, 512], P('row', 'col'), may hold values from 0 to 7
- pad_class: int32 [1024, 512], P('row', 'col'), may hold values from 0 to 7
- edge_table: float32 [8], replicated, may hold values from 0.5 to 4
- pad_table: float32 [8], replicated, may hold values from 0.02 to 0.5
Outputs:
- solution: float32 [32, 1024, 512], P(None, 'row', 'col')
- residual: float32 [32, 1024, 512], P(None, 'row', 'col')
The draws below stay inside these ranges and needn't reach their ends.
Inputs may be any that keep to these rules, and one draw needn't show every extreme that they name: `labels`: every number from 0 to 255 is the label of some nodes; the label of node (i, j) is 16 * floor(16 * i2 / 1024) + floor(16 * j2 / 512) for some node (i2, j2) of the grid with |i2 - i| <= 16 and |j2 - j| <= 8.
All inputs are finite; a program needn't handle non-finite values.
Results may differ from the reference program's by a relative error of at most 0.0003.
Values sent between devices are 32-bit elements; how exact they have to be, the bound alone decides.
A program may use at most 128 MiB of HBM per device.

```python
import math
from functools import partial
import jax
import jax.numpy as jnp
from jax import lax

NRHS = 32
REG = 16
NCLS = 8
ITERS = 2
NX = 1024
NY = 512


def draw_labels(key, part):
    first_key, second_key = jax.random.split(jax.random.fold_in(key, 17))
    reach_rows = NX // (4 * REG)
    reach_cols = NY // (4 * REG)
    row_shift = jax.random.randint(first_key, (NX, NY), -reach_rows, reach_rows + 1)
    col_shift = jax.random.randint(second_key, (NX, NY), -reach_cols, reach_cols + 1)
    rows_index = jnp.arange(NX, dtype=jnp.int32)[:, None] + row_shift
    columns = jnp.arange(NY, dtype=jnp.int32)[None, :] + col_shift
    row_block = jnp.clip(rows_index * REG // NX, 0, REG - 1)
    col_block = jnp.clip(columns * REG // NY, 0, REG - 1)
    return (row_block * REG + col_block).astype(jnp.int32)


def draw_load_currents(key, part):
    rows_index = jnp.arange(NX, dtype=jnp.float32)[:, None]
    rising = 1.0 + 2.0 * rows_index / max(NX - 1, 1)
    normal_part = jnp.clip(jax.random.normal(jax.random.fold_in(key, 5), (NRHS, NX, NY), jnp.float32), -6.0, 6.0)
    return 2.0 * normal_part * rising


def set_ends(entries, own_key, low, largest):
    longest = entries.shape.index(max(entries.shape))
    spots = []
    for shift in (0, 1):
        where = [jax.random.randint(jax.random.fold_in(own_key, axis), (), 0, length) for axis, length in enumerate(entries.shape)]
        where[longest] = (where[longest] + shift) % entries.shape[longest]
        spots.append(tuple(where))
    return entries.at[spots[0]].set(low).at[spots[1]].set(largest)


def steps_of(own_key, dims, pieces, smallest, top_value):
    level, own = 1.0, jax.random.fold_in(own_key, 6)
    for axis_at, parts in pieces:
        steps = jnp.exp(jax.random.uniform(jax.random.fold_in(own, axis_at), (parts,), jnp.float32, smallest / len(pieces), top_value / len(pieces)))
        level = level * jnp.repeat(steps, dims[axis_at] // parts).reshape([-1 if axis == axis_at else 1 for axis in range(len(dims))])
    return level


def setup_inputs(seed: int = 0) -> dict:
    splits = jax.random.split(jax.random.key(seed), 9)
    load_currents = draw_load_currents(jax.random.fold_in(splits[8], 71), 0)
    labels = draw_labels(jax.random.fold_in(splits[8], 71), 0)
    bump_height = jnp.clip(jnp.exp(math.log(2.0) - 1.3862944 * jax.random.uniform(splits[2], (NX, NY), jnp.float32) ** steps_of(splits[2], (NX, NY), ((0, 8), (1, 4)), -0.2, 0.2)), 0.5, 2.0)
    horizontal_class = set_ends(jax.random.randint(splits[3], (NX, NY), 0, NCLS), jax.random.fold_in(splits[3], 1), 0, NCLS - 1).astype(jnp.int32)
    vertical_class = set_ends(jax.random.randint(splits[4], (NX, NY), 0, NCLS), jax.random.fold_in(splits[4], 1), 0, NCLS - 1).astype(jnp.int32)
    pad_class = set_ends(jax.random.randint(splits[5], (NX, NY), 0, NCLS), jax.random.fold_in(splits[5], 1), 0, NCLS - 1).astype(jnp.int32)
    edge_table = jnp.clip(jnp.exp(jax.random.uniform(splits[6], (NCLS,), jnp.float32, math.log(0.5), math.log(4.0))), 0.5, 4.0)
    pad_table = jnp.clip(jnp.exp(jax.random.uniform(splits[7], (NCLS,), jnp.float32, math.log(0.02), math.log(0.5))), 0.02, 0.5)
    return {"load_currents": load_currents, "labels": labels, "bump_height": bump_height, "horizontal_class": horizontal_class, "vertical_class": vertical_class, "pad_class": pad_class, "edge_table": edge_table, "pad_table": pad_table}


precise = lax.Precision.HIGHEST

def link_fields(horizontal_class, vertical_class, edge_table):
    right_link = edge_table[horizontal_class]
    down_link = edge_table[vertical_class]
    columns = lax.broadcasted_iota(jnp.int32, horizontal_class.shape, 1)
    rows_index = lax.broadcasted_iota(jnp.int32, horizontal_class.shape, 0)
    right_link = jnp.where(columns == horizontal_class.shape[1] - 1, 0.0, right_link)
    down_link = jnp.where(rows_index == horizontal_class.shape[0] - 1, 0.0, down_link)
    left_link = jnp.pad(right_link, ((0, 0), (1, 0)))[:, :-1]
    upper_link = jnp.pad(down_link, ((1, 0), (0, 0)))[:-1, :]
    return (right_link, left_link, down_link, upper_link)

def apply_operator(field, coeffs):
    diagonal, right_link, left_link, down_link, upper_link = coeffs
    padded = jnp.pad(field, 1)
    return diagonal * field - right_link * padded[1:-1, 2:] - left_link * padded[1:-1, :-2] - down_link * padded[2:, 1:-1] - upper_link * padded[:-2, 1:-1]

def assemble_coarse(labels, bump_height, coeffs, regions):
    diagonal, right_link, left_link, down_link, upper_link = coeffs
    right_label = jnp.roll(labels, -1, axis=1)
    right_bump = jnp.roll(bump_height, -1, axis=1)
    down_label = jnp.roll(labels, -1, axis=0)
    down_bump = jnp.roll(bump_height, -1, axis=0)
    pair_ids = jnp.concatenate([(labels * regions + labels).reshape(-1), (labels * regions + right_label).reshape(-1), (right_label * regions + labels).reshape(-1), (labels * regions + down_label).reshape(-1), (down_label * regions + labels).reshape(-1)]).astype(jnp.int32)
    across = -(right_link * bump_height * right_bump)
    downward = -(down_link * bump_height * down_bump)
    weights = jnp.concatenate([(diagonal * bump_height * bump_height).reshape(-1), across.reshape(-1), across.reshape(-1), downward.reshape(-1), downward.reshape(-1)])
    summed = jax.ops.segment_sum(weights, pair_ids, num_segments=regions * regions)
    return summed.reshape(regions, regions)

def invert(matrix):
    factor = jnp.linalg.cholesky(matrix)
    identity = jnp.eye(matrix.shape[0], dtype=matrix.dtype)
    lower_solved = lax.linalg.triangular_solve(factor, identity, left_side=True, lower=True)
    return lax.linalg.triangular_solve(factor, lower_solved, left_side=True, lower=True, transpose_a=True)

def solve_single(single_load, labels, bump_height, coeffs, inverse, regions):
    flat_labels = labels.reshape(-1).astype(jnp.int32)
    diagonal = coeffs[0]

    def project(field):
        return jax.ops.segment_sum((bump_height * field).reshape(-1), flat_labels, num_segments=regions)

    def expand(coarse):
        return bump_height * jnp.take(coarse, labels, axis=0)

    def solve_coarse(projected):
        return jnp.dot(projected, inverse, precision=precise)

    def refresh(residual):
        scaled = residual / diagonal
        weighted_norm = jnp.sum(residual * scaled)
        field_image = apply_operator(scaled, coeffs)
        coarse = solve_coarse(project(field_image))
        return (scaled, weighted_norm, field_image, coarse)
    solution = expand(solve_coarse(project(single_load)))
    residual = single_load - apply_operator(solution, coeffs)
    scaled, weighted_norm, field_image, coarse = refresh(residual)
    spread = expand(coarse)
    direction = scaled - spread
    direction_image = field_image - apply_operator(spread, coeffs)
    for iteration in range(ITERS):
        step_size = weighted_norm / jnp.sum(direction * direction_image)
        solution = solution + step_size * direction
        residual = residual - step_size * direction_image
        if iteration + 1 < ITERS:
            scaled, new_norm, field_image, coarse = refresh(residual)
            spread = expand(coarse)
            beta_ratio = new_norm / weighted_norm
            direction = scaled - spread + beta_ratio * direction
            direction_image = field_image - apply_operator(spread, coeffs) + beta_ratio * direction_image
            weighted_norm = new_norm
    return (solution, residual)

def reference(load_currents, labels, bump_height, horizontal_class, vertical_class, pad_class, edge_table, pad_table):
    right_link, left_link, down_link, upper_link = link_fields(horizontal_class, vertical_class, edge_table)
    diagonal = pad_table[pad_class] + right_link + left_link + down_link + upper_link
    coeffs = (diagonal, right_link, left_link, down_link, upper_link)
    regions = REG * REG
    inverse = invert(assemble_coarse(labels, bump_height, coeffs, regions))
    worker = partial(solve_single, labels=labels, bump_height=bump_height, coeffs=coeffs, inverse=inverse, regions=regions)
    solution, residual = lax.map(worker, load_currents)
    return (solution, residual)
```

```python
import functools

import jax
import jax.numpy as jnp
from jax import lax
from jax.experimental import pallas as pl
from jax.experimental.pallas import tpu as pltpu
from jax.sharding import PartitionSpec as P

REG = 16
F32 = jnp.float32
precise = lax.Precision.HIGHEST
VM = pl.BlockSpec(memory_space=pltpu.VMEM)
PARAMS = pltpu.CompilerParams(vmem_limit_bytes=56 * 1024 * 1024)


def shape(*dims):
    return jax.ShapeDtypeStruct(dims, F32)


def shifted(value, axis, steps):
    count = lax.axis_size(axis)
    initial, last = (max(0, -steps), min(count, count - steps))
    return lax.ppermute(value, axis, [(i, i + steps) for i in range(initial, last)])


def lookup(entries, classes):
    out = jnp.zeros(classes.shape, F32)
    for k in range(entries.shape[0]):
        out = jnp.where(classes == k, entries[k], out)
    return out


def sweep(size, out_ref):
    lanes = lax.broadcasted_iota(jnp.int32, (size, size), 1)
    rows = lax.broadcasted_iota(jnp.int32, (size, 1), 0)
    row_lanes = lax.broadcasted_iota(jnp.int32, (1, size), 1)

    def step(k, carry):
        matrix = out_ref[...]
        row = out_ref[pl.ds(k, 1), :]
        pivot = jnp.sum(jnp.where(row_lanes == k, row, 0.0), axis=1, keepdims=True)
        col = jnp.sum(jnp.where(lanes == k, matrix, 0.0), axis=1, keepdims=True)
        recip = 1.0 / pivot
        scaled = jnp.where(row_lanes == k, recip, row * recip)
        kept = jnp.where(lanes == k, 0.0, matrix)
        out_ref[...] = kept - jnp.where(rows == k, 0.0, col) * scaled
        out_ref[pl.ds(k, 1), :] = scaled
        return carry

    lax.fori_loop(0, size, step, 0)


BLOCK = 32


def fold(value):
    half = value + pltpu.roll(value, 2 * BLOCK, 1)
    return half + pltpu.roll(half, BLOCK, 1)


def split_dot(exact, value, contract):
    total = None
    for _ in range(3):
        part = value.astype(jnp.bfloat16)
        value = value - part.astype(F32)
        term = lax.dot_general(*((exact, part) if contract[2] else (part, exact)), (contract[:2], ((), ())), preferred_element_type=F32)
        total = term if total is None else total + term
    return total


def pack(hot_ref, sums, dots=()):
    out = None
    for b in (0, 1):
        term = lax.dot_general(hot_ref[b], sums[b], (((1,), (1,)), ((), ())), precision=precise, preferred_element_type=F32)
        out = term if out is None else out + term
    if dots:
        sub = lax.broadcasted_iota(jnp.int32, out.shape, 0)
        ends = jnp.concatenate(list(dots), axis=0)
        full = sums[0].shape[0]
        if ends.shape[0] < full:
            ends = jnp.concatenate([ends, jnp.zeros((full - ends.shape[0], ends.shape[1]), F32)], axis=0)
        total = lax.dot_general(jnp.ones(out.shape[:1] + ends.shape[1:], F32), ends, (((1,), (1,)), ((), ())), precision=precise, preferred_element_type=F32)
        out = jnp.where(sub == out.shape[0] - 1, total, out)
    return out


def unpack(place_ref, gathered):
    block = lax.broadcasted_iota(jnp.int32, gathered.shape, 1) // BLOCK
    stacked = jnp.concatenate([jnp.where(block == k, gathered, 0.0) for k in range(4)], axis=0)
    return fold(split_dot(place_ref[...], stacked, ((1,), (0,), True)))


def gather_kernel(rows, cols, x_ref, out_ref, send_sem, recv_sem):
    count = rows * cols
    me = lax.axis_index("row") * cols + lax.axis_index("col")
    barrier = pltpu.get_barrier_semaphore()

    def target(d):
        other = lax.rem(me + d, count)
        return (other // cols, lax.rem(other, cols))

    def greet(d, carry):
        pl.semaphore_signal(barrier, inc=1, device_id=target(d), device_id_type=pl.DeviceIdType.MESH)
        return carry

    lax.fori_loop(1, count, greet, 0)
    pl.semaphore_wait(barrier, count - 1)

    def copy(d):
        return pltpu.make_async_remote_copy(
            src_ref=x_ref,
            dst_ref=out_ref.at[me],
            send_sem=send_sem.at[d],
            recv_sem=recv_sem.at[d],
            device_id=target(d),
            device_id_type=pl.DeviceIdType.MESH,
        )

    def send(d, carry):
        copy(d).start()
        return carry

    def finish(d, carry):
        copy(d).wait()
        return carry

    lax.fori_loop(1, count, send, 0)
    out_ref[pl.ds(me, 1)] = x_ref[...][None]
    lax.fori_loop(1, count, finish, 0)


def gather(value, ident):
    rows, cols = lax.axis_size("row"), lax.axis_size("col")
    count = rows * cols
    return pl.pallas_call(
        functools.partial(gather_kernel, rows, cols),
        out_shape=shape(count, *value.shape),
        in_specs=[VM],
        out_specs=VM,
        scratch_shapes=[pltpu.SemaphoreType.DMA((count,)), pltpu.SemaphoreType.DMA((count,))],
        compiler_params=pltpu.CompilerParams(collective_id=ident, has_side_effects=True),
    )(value)


def exchange_kernel(rows, cols, *refs):
    sources, landed, (send_sem, recv_sem) = refs[:4], refs[4:8], refs[8:]
    r, c = lax.axis_index("row"), lax.axis_index("col")
    targets = (
        (lax.rem(r + 1, rows), c),
        (lax.rem(r + rows - 1, rows), c),
        (r, lax.rem(c + 1, cols)),
        (r, lax.rem(c + cols - 1, cols)),
    )
    barrier = pltpu.get_barrier_semaphore()
    for target in targets:
        pl.semaphore_signal(barrier, inc=1, device_id=target, device_id_type=pl.DeviceIdType.MESH)
    pl.semaphore_wait(barrier, 4)
    copies = [
        pltpu.make_async_remote_copy(
            src_ref=sources[k],
            dst_ref=landed[k],
            send_sem=send_sem.at[k],
            recv_sem=recv_sem.at[k],
            device_id=targets[k],
            device_id_type=pl.DeviceIdType.MESH,
        )
        for k in range(4)
    ]
    for copy in copies:
        copy.start()
    for copy in copies:
        copy.wait()


def exchange(values, ident):
    return pl.pallas_call(
        functools.partial(exchange_kernel, lax.axis_size("row"), lax.axis_size("col")),
        out_shape=tuple(shape(*v.shape) for v in values),
        in_specs=[VM] * 4,
        out_specs=(VM,) * 4,
        scratch_shapes=[pltpu.SemaphoreType.DMA((4,)), pltpu.SemaphoreType.DMA((4,))],
        compiler_params=pltpu.CompilerParams(collective_id=ident, has_side_effects=True),
    )(*values)


def matrix_kernel(plan, gathered_ref, place_ref, out_ref):
    diagonals = unpack(place_ref, gathered_ref[...])
    size = out_ref.shape[0]
    gap = lax.broadcasted_iota(jnp.int32, (size, size), 1) - lax.broadcasted_iota(jnp.int32, (size, size), 0)
    total = jnp.zeros((size, size), F32)
    for k in range(9):
        total = jnp.where(gap == REG * (k // 3 - 1) + k % 3 - 1, diagonals[:, k : k + 1], total)
    out_ref[...] = total
    sweep(size, out_ref)


def coarse_of(gathered, place_ref, inverse_ref):
    sums = unpack(place_ref, gathered)
    coarse = jnp.dot(inverse_ref[...], sums, precision=precise, preferred_element_type=F32)
    return sums, coarse


def expand_into(out_ref, coarse, expand_ref):
    near = split_dot(expand_ref[...], coarse, ((0,), (0,), False))
    loads = BLOCK
    cols = out_ref.shape[-1]
    levels = out_ref.shape[1] // loads
    for b in (0, 1):
        for l in range(levels):
            k = b * levels + l
            out_ref[b, l * loads : (l + 1) * loads, :] = near[:loads, k * cols : (k + 1) * cols]


def wide(value):
    return jnp.broadcast_to(value, (value.shape[1],) * 2).T[:BLOCK]


def totals(gathered_ref, count):
    summed = jnp.sum(gathered_ref[...].reshape(-1, 8, gathered_ref.shape[-1]), axis=0)[7:8]
    block = lax.broadcasted_iota(jnp.int32, summed.shape, 1) // BLOCK
    return [fold(jnp.where(block == k, summed, 0.0)) for k in range(count)]


def solve_first(plan, gathered_ref, place_ref, inverse_ref, expand_ref, cx_ref, c_ref):
    _, coarse = coarse_of(gathered_ref[...], place_ref, inverse_ref)
    c_ref[...] = coarse
    expand_into(cx_ref, coarse, expand_ref)


def solve_second(plan, gathered_ref, place_ref, inverse_ref, expand_ref, cx_ref, c_ref, scal_ref, alpha_ref):
    sums, coarse = coarse_of(gathered_ref[...], place_ref, inverse_ref)
    rho, image_dot = totals(gathered_ref, 2)
    curve = image_dot - jnp.sum(coarse * sums, axis=0, keepdims=True)
    alpha = rho / curve
    c_ref[...] = coarse
    scal_ref[0:1] = rho
    scal_ref[1:2] = curve
    scal_ref[2:3] = alpha
    alpha_ref[...] = wide(alpha)
    expand_into(cx_ref, coarse, expand_ref)


def solve_third(plan, gathered_ref, place_ref, inverse_ref, expand_ref, c0_ref, c1_ref, scal_ref, cs_ref, cx_ref, out_ref):
    sums, coarse = coarse_of(gathered_ref[...], place_ref, inverse_ref)
    rho1, qz, image_dot = totals(gathered_ref, 3)
    rho, curve, alpha0 = scal_ref[0:1], scal_ref[1:2], scal_ref[2:3]
    beta = rho1 / rho
    curve1 = image_dot - jnp.sum(coarse * sums, axis=0, keepdims=True) + 2.0 * beta * qz + beta * beta * curve
    alpha1 = rho1 / curve1
    mix = alpha0 + alpha1 * beta
    expand_into(cx_ref, coarse, expand_ref)
    expand_into(cs_ref, c0_ref[...] - alpha1 * coarse - mix * c1_ref[...], expand_ref)
    out_ref[0] = wide(mix)
    out_ref[1] = wide(alpha1)
    out_ref[2] = wide(beta)


class Plan:
    def __init__(self, rows, loads, height):
        self.rows, self.loads, self.height = rows, loads, height
        self.parts = rows // height + 1
        self.levels = self.parts + 1

    def chunks(self):
        half = self.height // 2
        for part in range(self.parts):
            yield part, max(0, part * self.height - half), min(self.rows, part * self.height + half)


def over_rows(first, last, step, init, group=4):
    def body(g, carry):
        for u in range(group):
            carry = step(first + g * group + u, carry)
        return carry

    return lax.fori_loop(0, (last - first) // group, body, init)


def row_of(ref, k, i):
    return ref[k, pl.ds(i, 1), :]


def spread(mask_ref, cx, i):
    out = row_of(mask_ref, 0, i) * cx[0]
    for k in range(1, 4):
        out = out + row_of(mask_ref, k, i) * cx[k]
    return out


def expansions(plan, cx_ref, part):
    n = plan.loads
    return [cx_ref[b, (part + a) * n : (part + a + 1) * n, :] for a in (0, 1) for b in (0, 1)]


def sums_kernel(plan, b_ref, mask_ref, image_ref, hot_ref, out_ref, s_ref, pair_ref):
    n = plan.loads
    s_ref[...] = jnp.zeros_like(s_ref)
    for part, first, last in plan.chunks():
        def step(i, acc):
            v = b_ref[pl.ds(i, n, stride=plan.rows), :]
            return tuple(x + row_of(mask_ref, k, i) * v for k, x in enumerate(acc))

        acc = over_rows(first, last, step, (jnp.zeros((n, s_ref.shape[-1]), F32),) * 4)
        add_sums(plan, s_ref, part, acc)
    out_ref[0] = pack(hot_ref, s_ref)
    pair_ref[...] = jnp.zeros_like(pair_ref)
    for part, first, last in plan.chunks():
        for k in range(4):
            for m in range(4):
                da, db = m // 2 - k // 2, m % 2 - k % 2
                at = (part + k // 2) * BLOCK + (da + 1) * 3 + db + 1
                term = jnp.sum(mask_ref[k, first:last, :] * image_ref[m, first:last, :], axis=0, keepdims=True)
                pair_ref[k % 2, at : at + 1, :] = pair_ref[k % 2, at : at + 1, :] + term
    out_ref[1] = pack(hot_ref, pair_ref)


def add_sums(plan, s_ref, part, acc):
    n = plan.loads
    for a in (0, 1):
        for b in (0, 1):
            where = slice((part + a) * n, (part + a + 1) * n)
            s_ref[b, where, :] = s_ref[b, where, :] + acc[2 * a + b]


def pack_edges(edges, z, i, cols):
    left, right = edges
    lane = lax.broadcasted_iota(jnp.int32, z.shape, 1)
    left = jnp.where(lane == i, pltpu.roll(z, i, 1), left)
    right = jnp.where(lane == i, pltpu.roll(z, lax.rem(i + 1, z.shape[1]), 1), right)
    return left, right


def first_kernel(plan, b_ref, image_ref, coef_ref, cx_ref, r_ref, z_ref, rho_ref, edge_ref):
    n = plan.loads
    zero = jnp.zeros((n, b_ref.shape[-1]), F32)
    carry = (zero, zero, zero)
    for part, first, last in plan.chunks():
        cx = expansions(plan, cx_ref, part)

        def step(i, carry):
            rho, *edges = carry
            r = b_ref[pl.ds(i, n, stride=plan.rows), :] - spread(image_ref, cx, i)
            z = r / row_of(coef_ref, 0, i)
            at = pl.ds(pl.multiple_of(i * n, n), n)
            r_ref[at, :] = r
            z_ref[at, :] = z
            return (rho + r * z, *pack_edges(edges, z, i, z.shape[1]))

        carry = over_rows(first, last, step, carry)
    rho_ref[0] = carry[0]
    edge_ref[0] = carry[1]
    edge_ref[1] = carry[2]


def image_kernel(plan, z_ref, above_ref, below_ref, left_ref, right_ref, coef_ref, mask_ref, hot_ref, dots_ref, f_ref, out_ref, s_ref):
    n = plan.loads
    cols = z_ref.shape[-1]
    zero = jnp.zeros((n, cols), F32)
    lane = lax.broadcasted_iota(jnp.int32, (n, cols), 1)
    s_ref[...] = jnp.zeros_like(s_ref)
    left_pack, right_pack = left_ref[...], right_ref[...]

    def image(i, z, up, down):
        before = jnp.where(lane == 0, pltpu.roll(left_pack, lax.rem(cols - i, cols), 1), pltpu.roll(z, 1, 1))
        after = jnp.where(lane == cols - 1, pltpu.roll(right_pack, cols - 1 - i, 1), pltpu.roll(z, cols - 1, 1))
        return (
            row_of(coef_ref, 0, i) * z
            - row_of(coef_ref, 1, i) * after
            - row_of(coef_ref, 2, i) * before
            - row_of(coef_ref, 3, i) * down
            - row_of(coef_ref, 4, i) * up
        )

    def load(i):
        return z_ref[pl.ds(pl.multiple_of(i * n, n), n), :]

    def step(i, carry):
        return finish(i, load(i), load(i - 1), load(i + 1), carry)

    def finish(i, z, up, down, carry):
        f = image(i, z, up, down)
        f_ref[pl.ds(pl.multiple_of(i * n, n), n), :] = f
        zf, *acc = carry
        return (zf + z * f, *[x + row_of(mask_ref, k, i) * f for k, x in enumerate(acc)])

    zf = zero
    for part, first, last in plan.chunks():
        carry = (zf,) + (zero,) * 4
        low, high = first, last
        if first == 0:
            carry = finish(0, load(0), above_ref[...], load(1), carry)
            low = 1
        if last == plan.rows:
            high = last - 1
        carry = over_rows(low, high, step, carry, 1 if (high - low) % 4 else 4)
        if last == plan.rows:
            carry = finish(last - 1, load(last - 1), load(last - 2), below_ref[...], carry)
        zf, *acc = carry
        add_sums(plan, s_ref, part, acc)
    out_ref[...] = pack(hot_ref, s_ref, [dots_ref[k] for k in range(dots_ref.shape[0])] + [zf])


def second_kernel(plan, r_ref, f_ref, image_ref, coef_ref, cx_ref, alpha_ref, r1_ref, z1_ref, q_ref, dots_ref, edge_ref):
    n = plan.loads
    zero = jnp.zeros((n, r_ref.shape[-1]), F32)
    carry = (zero,) * 4
    alpha = alpha_ref[...]
    for part, first, last in plan.chunks():
        cx = expansions(plan, cx_ref, part)

        def step(i, carry):
            rho, qz, *edges = carry
            at = pl.ds(pl.multiple_of(i * n, n), n)
            q = f_ref[at, :] - spread(image_ref, cx, i)
            r = r_ref[at, :] - alpha * q
            z = r / row_of(coef_ref, 0, i)
            q_ref[at, :] = q
            r1_ref[at, :] = r
            z1_ref[at, :] = z
            return (rho + r * z, qz + q * z, *pack_edges(edges, z, i, z.shape[1]))

        carry = over_rows(first, last, step, carry)
    dots_ref[0] = carry[0]
    dots_ref[1] = carry[1]
    edge_ref[0] = carry[2]
    edge_ref[1] = carry[3]


def last_kernel(plan, z_ref, z1_ref, r1_ref, f1_ref, q_ref, mask_ref, image_ref, cs_ref, cx_ref, scal_ref, s_out, r_out):
    n = plan.loads
    mix, alpha, beta = scal_ref[0], scal_ref[1], scal_ref[2]
    for part, first, last in plan.chunks():
        cs = expansions(plan, cs_ref, part)
        cx = expansions(plan, cx_ref, part)

        def step(i, carry):
            at = pl.ds(pl.multiple_of(i * n, n), n)
            to = pl.ds(i, n, stride=plan.rows)
            s_out[to, :] = spread(mask_ref, cs, i) + mix * z_ref[at, :] + alpha * z1_ref[at, :]
            q1 = f1_ref[at, :] - spread(image_ref, cx, i) + beta * q_ref[at, :]
            r_out[to, :] = r1_ref[at, :] - alpha * q1
            return carry

        over_rows(first, last, step, 0, 2)


def body(load_currents, labels, bump_height, horizontal_class, vertical_class, pad_class, edge_table, pad_table):
    rows, cols = labels.shape
    loads = load_currents.shape[0]
    regions = REG * REG
    grid_rows = lax.axis_size("row") * rows
    grid_cols = lax.axis_size("col") * cols
    height, width = grid_rows // REG, grid_cols // REG
    plan = Plan(rows, loads, height)
    levels = plan.levels
    ri, ci = lax.axis_index("row"), lax.axis_index("col")
    row_ids = ri * rows + lax.broadcasted_iota(jnp.int32, (rows, cols), 0)
    col_ids = ci * cols + lax.broadcasted_iota(jnp.int32, (rows, cols), 1)
    right_link = jnp.where(col_ids == grid_cols - 1, 0.0, lookup(edge_table, horizontal_class))
    down_link = jnp.where(row_ids == grid_rows - 1, 0.0, lookup(edge_table, vertical_class))
    named = labels.astype(F32)
    right_end = jnp.stack([named[:, -1], bump_height[:, -1], right_link[:, -1]])
    left_end = jnp.stack([named[:, 0], bump_height[:, 0]])
    low_end = jnp.stack([named[-1], bump_height[-1], down_link[-1]])
    top_end = jnp.stack([named[0], bump_height[0]])
    before = shifted(right_end, "col", 1)
    after = shifted(left_end, "col", -1)
    above = shifted(low_end, "row", 1)
    below = shifted(top_end, "row", -1)

    def at_left(value, k):
        return jnp.concatenate([before[k][:, None], value[:, :-1]], axis=1)

    def at_right(value, k):
        return jnp.concatenate([value[:, 1:], after[k][:, None]], axis=1)

    def at_top(value, k):
        return jnp.concatenate([above[k][None], value[:-1]], axis=0)

    def at_low(value, k):
        return jnp.concatenate([value[1:], below[k][None]], axis=0)

    left_link = at_left(right_link, 2)
    upper_link = at_top(down_link, 2)
    diagonal = lookup(pad_table, pad_class) + right_link + left_link + down_link + upper_link
    base_row = (row_ids + height // 2) // height - 1
    base_col = (col_ids + width // 2) // width - 1

    def masks(name, weight):
        name = name.astype(jnp.int32)
        a, b = name // REG - base_row, name % REG - base_col
        return jnp.stack([jnp.where((a == i) & (b == j), weight, 0.0) for i in (0, 1) for j in (0, 1)])

    mask = masks(named, bump_height)
    image = (
        masks(named, diagonal * bump_height)
        - masks(at_right(named, 0), right_link * at_right(bump_height, 1))
        - masks(at_left(named, 0), left_link * at_left(bump_height, 1))
        - masks(at_low(named, 0), down_link * at_low(bump_height, 1))
        - masks(at_top(named, 0), upper_link * at_top(bump_height, 1))
    )
    coef = jnp.stack([diagonal, right_link, left_link, down_link, upper_link])

    span = cols // width + 2
    lane_base = (lax.iota(jnp.int32, cols) + width // 2) // width
    hot = jnp.stack([(lane_base[None] + b == lax.iota(jnp.int32, 8)[:, None]).astype(F32) for b in (0, 1)])
    count = lax.axis_size("row") * lax.axis_size("col")
    here = lax.broadcasted_iota(jnp.int32, (regions, 4 * count * 8), 0)
    sent = lax.broadcasted_iota(jnp.int32, (regions, 4 * count * 8), 1)
    level, device, x = sent // (count * 8), sent // 8 % count, sent % 8
    at_row = device // lax.axis_size("col") * (rows // height) - 1 + level
    at_col = device % lax.axis_size("col") * (cols // width) - 1 + x
    place = ((here // REG == at_row) & (here % REG == at_col) & (x < span) & (level < levels)).astype(jnp.bfloat16)
    here = lax.broadcasted_iota(jnp.int32, (regions, 2 * levels * cols), 0)
    lane = lax.broadcasted_iota(jnp.int32, (regions, 2 * levels * cols), 1)
    which, lane = lane // cols, lane % cols
    at_row = ri * (rows // height) - 1 + which % levels
    at_col = ci * (cols // width) - 1 + (lane + width // 2) // width + which // levels
    expand = ((here // REG == at_row) & (here % REG == at_col)).astype(jnp.bfloat16)

    def call(kernel, outs, *args, scratch=()):
        return pl.pallas_call(
            functools.partial(kernel, plan),
            out_shape=outs,
            in_specs=[VM] * len(args),
            out_specs=jax.tree.map(lambda _: VM, outs),
            scratch_shapes=scratch,
            compiler_params=PARAMS,
        )(*args)

    s_shape = shape(2, levels * loads, cols)
    sums_scratch = [pltpu.VMEM((2, 4 * BLOCK, cols), F32)]
    field = shape(rows * loads, cols)
    message = shape(8, 4 * BLOCK)
    coarse_shape = shape(regions, 4 * BLOCK)

    def image_of(z, edges, dots, ident):
        landed = exchange((z[-loads:], z[:loads], edges[1], edges[0]), ident)
        f, sums = call(image_kernel, (field, message), z, *landed, coef, mask, hot, dots, scratch=sums_scratch)
        return f, gather(sums, ident + 1).reshape(count * 8, 4 * BLOCK)

    flat = load_currents.reshape(loads * rows, cols)
    first = call(sums_kernel, shape(2, 8, 4 * BLOCK), flat, mask, image, hot, scratch=sums_scratch * 2)
    first = gather(first, 0)
    inverse = call(matrix_kernel, shape(regions, regions), first[:, 1].reshape(count * 8, 4 * BLOCK), place)
    cx, c0 = call(solve_first, (s_shape, coarse_shape), first[:, 0].reshape(count * 8, 4 * BLOCK), place, inverse, expand)
    r0, z0, rho_lanes, edges = call(
        first_kernel, (field, field, shape(1, loads, cols), shape(2, loads, cols)), flat, image, coef, cx
    )
    f0, sums = image_of(z0, edges, rho_lanes, 1)
    cx, c1, scal, alpha = call(
        solve_second, (s_shape, coarse_shape, shape(8, 4 * BLOCK), shape(loads, cols)), sums, place, inverse, expand
    )
    r1, z1, q0, dots, edges = call(
        second_kernel,
        (field, field, field, shape(2, loads, cols), shape(2, loads, cols)),
        r0, f0, image, coef, cx, alpha,
    )
    f1, sums = image_of(z1, edges, dots, 3)
    cs, cx, scal = call(
        solve_third, (s_shape, s_shape, shape(3, loads, cols)), sums, place, inverse, expand, c0, c1, scal
    )
    s, r = call(
        last_kernel, (shape(loads * rows, cols),) * 2,
        z0, z1, r1, f1, q0, mask, image, cs, cx, scal,
    )
    return (s.reshape(load_currents.shape), r.reshape(load_currents.shape))


def solution(mesh):
    grid = P("row", "col")
    cube = P(None, "row", "col")
    return jax.shard_map(
        body,
        mesh=mesh,
        in_specs=(cube, grid, grid, grid, grid, grid, P(), P()),
        out_specs=(cube, cube),
        check_vma=False,
    )
```

```python
import functools

import jax
import jax.numpy as jnp
from jax import lax
from jax.experimental import pallas as pl
from jax.experimental.pallas import tpu as pltpu
from jax.sharding import PartitionSpec as P

REG = 16
F32 = jnp.float32
precise = lax.Precision.HIGHEST
VM = pl.BlockSpec(memory_space=pltpu.VMEM)
PARAMS = pltpu.CompilerParams(vmem_limit_bytes=56 * 1024 * 1024)


def shape(*dims):
    return jax.ShapeDtypeStruct(dims, F32)


def sweep(size, out_ref):
    segment = 2 * REG
    for start in range(0, size, segment):
        reach = min(size, start + segment + 2 * REG)
        width = size
        lanes = lax.broadcasted_iota(jnp.int32, (reach, width), 1)
        rows = lax.broadcasted_iota(jnp.int32, (reach, 1), 0)
        row_lanes = lax.broadcasted_iota(jnp.int32, (1, width), 1)

        def step(k, carry, reach=reach, width=width, lanes=lanes, rows=rows, row_lanes=row_lanes):
            matrix = out_ref[:reach, :]
            row = out_ref[pl.ds(k, 1), :]
            pivot = jnp.sum(jnp.where(row_lanes == k, row, 0.0), axis=1, keepdims=True)
            here = lanes == k
            col = jnp.sum(jnp.where(here, matrix, 0.0), axis=1, keepdims=True)
            recip = 1.0 / pivot
            scaled = jnp.where(row_lanes == k, recip, row * recip)
            out_ref[:reach, :] = jnp.where(here, 0.0, matrix) - jnp.where(rows == k, 0.0, col) * scaled
            out_ref[pl.ds(k, 1), :] = scaled
            return carry

        lax.fori_loop(start, min(size, start + segment), step, 0)


BLOCK = 32


def fold(value):
    half = value + pltpu.roll(value, 2 * BLOCK, 1)
    return half + pltpu.roll(half, BLOCK, 1)


def split_dot(exact, value, contract):
    total = None
    for _ in range(3):
        part = value.astype(jnp.bfloat16)
        value = value - part.astype(F32)
        term = lax.dot_general(*((exact, part) if contract[2] else (part, exact)), (contract[:2], ((), ())), preferred_element_type=F32)
        total = term if total is None else total + term
    return total


def pack(hot_ref, sums, dots=()):
    out = None
    for b in (0, 1):
        term = lax.dot_general(hot_ref[b], sums[b], (((1,), (1,)), ((), ())), precision=precise, preferred_element_type=F32)
        out = term if out is None else out + term
    if dots:
        sub = lax.broadcasted_iota(jnp.int32, out.shape, 0)
        ends = jnp.concatenate(list(dots), axis=0)
        full = sums[0].shape[0]
        if ends.shape[0] < full:
            ends = jnp.concatenate([ends, jnp.zeros((full - ends.shape[0], ends.shape[1]), F32)], axis=0)
        total = lax.dot_general(jnp.ones(out.shape[:1] + ends.shape[1:], F32), ends, (((1,), (1,)), ((), ())), precision=precise, preferred_element_type=F32)
        out = jnp.where(sub == out.shape[0] - 1, total, out)
    return out


def unpack(place_ref, gathered):
    block = lax.broadcasted_iota(jnp.int32, gathered.shape, 1) // BLOCK
    stacked = jnp.concatenate([jnp.where(block == k, gathered, 0.0) for k in range(4)], axis=0)
    return fold(split_dot(place_ref[...], stacked, ((1,), (0,), True)))


def gather_kernel(rows, cols, x_ref, out_ref, send_sem, recv_sem):
    count = rows * cols
    me = lax.axis_index("row") * cols + lax.axis_index("col")
    barrier = pltpu.get_barrier_semaphore()

    def target(d):
        other = lax.rem(me + d, count)
        return (other // cols, lax.rem(other, cols))

    def greet(d, carry):
        pl.semaphore_signal(barrier, inc=1, device_id=target(d), device_id_type=pl.DeviceIdType.MESH)
        return carry

    lax.fori_loop(1, count, greet, 0)
    pl.semaphore_wait(barrier, count - 1)

    def copy(d):
        return pltpu.make_async_remote_copy(
            src_ref=x_ref,
            dst_ref=out_ref.at[me],
            send_sem=send_sem.at[d],
            recv_sem=recv_sem.at[d],
            device_id=target(d),
            device_id_type=pl.DeviceIdType.MESH,
        )

    def send(d, carry):
        copy(d).start()
        return carry

    def finish(d, carry):
        copy(d).wait()
        return carry

    lax.fori_loop(1, count, send, 0)
    out_ref[pl.ds(me, 1)] = x_ref[...][None]
    lax.fori_loop(1, count, finish, 0)


def gather(value, ident):
    rows, cols = lax.axis_size("row"), lax.axis_size("col")
    count = rows * cols
    return pl.pallas_call(
        functools.partial(gather_kernel, rows, cols),
        out_shape=shape(count, *value.shape),
        in_specs=[VM],
        out_specs=VM,
        scratch_shapes=[pltpu.SemaphoreType.DMA((count,)), pltpu.SemaphoreType.DMA((count,))],
        compiler_params=pltpu.CompilerParams(collective_id=ident, has_side_effects=True),
    )(value)


def exchange_kernel(rows, cols, x_ref, out_ref, send_sem, recv_sem):
    r, c = lax.axis_index("row"), lax.axis_index("col")
    targets = (
        (lax.rem(r + 1, rows), c),
        (lax.rem(r + rows - 1, rows), c),
        (r, lax.rem(c + 1, cols)),
        (r, lax.rem(c + cols - 1, cols)),
    )
    barrier = pltpu.get_barrier_semaphore()
    for target in targets:
        pl.semaphore_signal(barrier, inc=1, device_id=target, device_id_type=pl.DeviceIdType.MESH)
    pl.semaphore_wait(barrier, 4)
    copies = [
        pltpu.make_async_remote_copy(
            src_ref=x_ref.at[k],
            dst_ref=out_ref.at[k],
            send_sem=send_sem.at[k],
            recv_sem=recv_sem.at[k],
            device_id=targets[k],
            device_id_type=pl.DeviceIdType.MESH,
        )
        for k in range(4)
    ]
    for copy in copies:
        copy.start()
    for copy in copies:
        copy.wait()


def exchange(value, ident):
    return pl.pallas_call(
        functools.partial(exchange_kernel, lax.axis_size("row"), lax.axis_size("col")),
        out_shape=shape(*value.shape),
        in_specs=[VM],
        out_specs=VM,
        scratch_shapes=[pltpu.SemaphoreType.DMA((4,)), pltpu.SemaphoreType.DMA((4,))],
        compiler_params=pltpu.CompilerParams(collective_id=ident, has_side_effects=True),
    )(value)


def matrix_kernel(plan, gathered_ref, place_ref, out_ref):
    diagonals = unpack(place_ref, gathered_ref[...])
    size = out_ref.shape[0]
    gap = lax.broadcasted_iota(jnp.int32, (size, size), 1) - lax.broadcasted_iota(jnp.int32, (size, size), 0)
    total = jnp.zeros((size, size), F32)
    for k in range(9):
        total = jnp.where(gap == REG * (k // 3 - 1) + k % 3 - 1, diagonals[:, k : k + 1], total)
    out_ref[...] = total
    sweep(size, out_ref)


def coarse_of(gathered, place_ref, inverse_ref):
    sums = unpack(place_ref, gathered)
    coarse = jnp.dot(inverse_ref[...], sums, precision=precise, preferred_element_type=F32)
    return sums, coarse


def expand_into(out_ref, coarse, expand_ref):
    near = split_dot(expand_ref[...], coarse, ((0,), (0,), False))
    loads = BLOCK
    cols = out_ref.shape[-1]
    levels = out_ref.shape[1] // loads
    for b in (0, 1):
        for l in range(levels):
            k = b * levels + l
            out_ref[b, l * loads : (l + 1) * loads, :] = near[:loads, k * cols : (k + 1) * cols]


def wide(value):
    return jnp.broadcast_to(value, (value.shape[1],) * 2).T[:BLOCK]


def totals(gathered_ref, count):
    summed = jnp.sum(gathered_ref[...].reshape(-1, 8, gathered_ref.shape[-1]), axis=0)[7:8]
    block = lax.broadcasted_iota(jnp.int32, summed.shape, 1) // BLOCK
    return [fold(jnp.where(block == k, summed, 0.0)) for k in range(count)]


def solve_first(plan, gathered_ref, place_ref, inverse_ref, expand_ref, cx_ref, c_ref):
    _, coarse = coarse_of(gathered_ref[...], place_ref, inverse_ref)
    c_ref[...] = coarse
    expand_into(cx_ref, coarse, expand_ref)


def solve_second(plan, gathered_ref, place_ref, inverse_ref, expand_ref, cx_ref, c_ref, scal_ref, alpha_ref):
    sums, coarse = coarse_of(gathered_ref[...], place_ref, inverse_ref)
    rho, image_dot = totals(gathered_ref, 2)
    curve = image_dot - jnp.sum(coarse * sums, axis=0, keepdims=True)
    alpha = rho / curve
    c_ref[...] = coarse
    scal_ref[0:1] = rho
    scal_ref[1:2] = curve
    scal_ref[2:3] = alpha
    alpha_ref[...] = wide(alpha)
    expand_into(cx_ref, coarse, expand_ref)


def solve_third(plan, gathered_ref, place_ref, inverse_ref, expand_ref, c0_ref, c1_ref, scal_ref, cs_ref, cx_ref, out_ref):
    sums, coarse = coarse_of(gathered_ref[...], place_ref, inverse_ref)
    rho1, qz, image_dot = totals(gathered_ref, 3)
    rho, curve, alpha0 = scal_ref[0:1], scal_ref[1:2], scal_ref[2:3]
    beta = rho1 / rho
    curve1 = image_dot - jnp.sum(coarse * sums, axis=0, keepdims=True) + 2.0 * beta * qz + beta * beta * curve
    alpha1 = rho1 / curve1
    mix = alpha0 + alpha1 * beta
    expand_into(cx_ref, coarse, expand_ref)
    expand_into(cs_ref, c0_ref[...] - alpha1 * coarse - mix * c1_ref[...], expand_ref)
    out_ref[0] = wide(mix)
    out_ref[1] = wide(alpha1)
    out_ref[2] = wide(beta)


class Plan:
    def __init__(self, rows, loads, height):
        self.rows, self.loads, self.height = rows, loads, height
        self.parts = rows // height + 1
        self.levels = self.parts + 1

    def chunks(self):
        half = self.height // 2
        for part in range(self.parts):
            yield part, max(0, part * self.height - half), min(self.rows, part * self.height + half)


def over_rows(first, last, step, init, group=4):
    def body(g, carry):
        for u in range(group):
            carry = step(first + g * group + u, carry)
        return carry

    return lax.fori_loop(0, (last - first) // group, body, init)


def row_of(ref, k, i):
    return ref[k, pl.ds(i, 1), :]


def spread(mask_ref, cx, i):
    out = row_of(mask_ref, 0, i) * cx[0]
    for k in range(1, 4):
        out = out + row_of(mask_ref, k, i) * cx[k]
    return out


def expansions(plan, cx_ref, part):
    n = plan.loads
    return [cx_ref[b, (part + a) * n : (part + a + 1) * n, :] for a in (0, 1) for b in (0, 1)]


def looked_up(table_ref, classes):
    out = jnp.zeros(classes.shape, F32)
    for k in range(table_ref.shape[0]):
        out = jnp.where(classes == k, table_ref[k], out)
    return out


def links_kernel(plan, h_ref, v_ref, label_ref, bump_ref, table_ref, link_ref, edge_ref):
    rows, cols = h_ref.shape
    last_row = lax.axis_index("row") == lax.axis_size("row") - 1
    last_col = lax.axis_index("col") == lax.axis_size("col") - 1
    i = lax.broadcasted_iota(jnp.int32, (rows, cols), 0)
    j = lax.broadcasted_iota(jnp.int32, (rows, cols), 1)
    row_end = jnp.where(last_row, rows - 1, rows)
    col_end = jnp.where(last_col, cols - 1, cols)
    right = jnp.where(j == col_end, 0.0, looked_up(table_ref, h_ref[...]))
    down = jnp.where(i == row_end, 0.0, looked_up(table_ref, v_ref[...]))
    link_ref[0] = right
    link_ref[1] = down
    edge_ref[...] = jnp.zeros_like(edge_ref)
    named = label_ref[...].astype(F32)
    bump = bump_ref[...]
    for k, value in enumerate((named, bump, down)):
        edge_ref[0, k : k + 1, :] = value[rows - 1 :]
        edge_ref[1, k : k + 1, :] = value[:1]
    for k, value in enumerate((named, bump, right)):
        turned = value.T
        edge_ref[2, k : k + 1, :] = turned[cols - 1 :]
        edge_ref[3, k : k + 1, :] = turned[:1]


def masks_kernel(plan, width, link_ref, edge_ref, label_ref, bump_ref, pad_ref, table_ref, mask_ref, image_ref, coef_ref):
    rows, cols = label_ref.shape
    i = lax.broadcasted_iota(jnp.int32, (rows, cols), 0)
    j = lax.broadcasted_iota(jnp.int32, (rows, cols), 1)

    def at_left(value, k):
        return jnp.where(j == 0, jnp.broadcast_to(edge_ref[2, k : k + 1, :], (cols, rows)).T, pltpu.roll(value, 1, 1))

    def at_right(value, k):
        return jnp.where(j == cols - 1, jnp.broadcast_to(edge_ref[3, k : k + 1, :], (cols, rows)).T, pltpu.roll(value, cols - 1, 1))

    def at_top(value, k):
        return jnp.where(i == 0, edge_ref[0, k : k + 1, :], pltpu.roll(value, 1, 0))

    def at_low(value, k):
        return jnp.where(i == rows - 1, edge_ref[1, k : k + 1, :], pltpu.roll(value, rows - 1, 0))

    right, down = link_ref[0], link_ref[1]
    left, upper = at_left(right, 2), at_top(down, 2)
    diagonal = looked_up(table_ref, pad_ref[...]) + right + left + down + upper
    for k, value in enumerate((diagonal, right, left, down, upper)):
        coef_ref[k] = value
    tile_row = (lax.axis_index("row") * (rows // plan.height) - 1).astype(F32)
    tile_col = (lax.axis_index("col") * (cols // width) - 1).astype(F32)
    base_row = jnp.zeros((rows, cols), F32) + tile_row
    base_col = jnp.zeros((rows, cols), F32) + tile_col
    for p in range(1, plan.parts):
        base_row = base_row + jnp.where(i >= p * plan.height - plan.height // 2, 1.0, 0.0)
    for p in range(1, cols // width + 1):
        base_col = base_col + jnp.where(j >= p * width - width // 2, 1.0, 0.0)
    named, bump = label_ref[...].astype(F32), bump_ref[...]
    total = None
    for label, weight in (
        (named, diagonal * bump),
        (at_right(named, 0), -right * at_right(bump, 1)),
        (at_left(named, 0), -left * at_left(bump, 1)),
        (at_low(named, 0), -down * at_low(bump, 1)),
        (at_top(named, 0), -upper * at_top(bump, 1)),
    ):
        high = jnp.floor(label * (1.0 / REG))
        a, b = high - base_row, label - REG * high - base_col
        hits = [(a == m) & (b == n) for m in (0.0, 1.0) for n in (0.0, 1.0)]
        if total is None:
            for k in range(4):
                mask_ref[k] = jnp.where(hits[k], bump, 0.0)
        terms = [jnp.where(hit, weight, 0.0) for hit in hits]
        total = terms if total is None else [t + u for t, u in zip(total, terms)]
    for k in range(4):
        image_ref[k] = total[k]


def sums_kernel(plan, b_ref, mask_ref, image_ref, hot_ref, out_ref, s_ref, pair_ref):
    n = plan.loads
    s_ref[...] = jnp.zeros_like(s_ref)
    for part, first, last in plan.chunks():
        def step(i, acc):
            v = b_ref[pl.ds(i, n, stride=plan.rows), :]
            return tuple(x + row_of(mask_ref, k, i) * v for k, x in enumerate(acc))

        acc = over_rows(first, last, step, (jnp.zeros((n, s_ref.shape[-1]), F32),) * 4)
        add_sums(plan, s_ref, part, acc)
    out_ref[0] = pack(hot_ref, s_ref)
    pair_ref[...] = jnp.zeros_like(pair_ref)
    for part, first, last in plan.chunks():
        for k in range(4):
            for m in range(4):
                da, db = m // 2 - k // 2, m % 2 - k % 2
                at = (part + k // 2) * BLOCK + (da + 1) * 3 + db + 1
                term = jnp.sum(mask_ref[k, first:last, :] * image_ref[m, first:last, :], axis=0, keepdims=True)
                pair_ref[k % 2, at : at + 1, :] = pair_ref[k % 2, at : at + 1, :] + term
    out_ref[1] = pack(hot_ref, pair_ref)


def add_sums(plan, s_ref, part, acc):
    n = plan.loads
    for a in (0, 1):
        for b in (0, 1):
            where = slice((part + a) * n, (part + a + 1) * n)
            s_ref[b, where, :] = s_ref[b, where, :] + acc[2 * a + b]


def pack_edges(edges, z, i, cols):
    left, right = edges
    lane = lax.broadcasted_iota(jnp.int32, z.shape, 1)
    left = jnp.where(lane == i, pltpu.roll(z, i, 1), left)
    right = jnp.where(lane == i, pltpu.roll(z, lax.rem(i + 1, z.shape[1]), 1), right)
    return left, right


def first_kernel(plan, b_ref, image_ref, coef_ref, cx_ref, r_ref, z_ref, rho_ref, edge_ref):
    n = plan.loads
    zero = jnp.zeros((n, b_ref.shape[-1]), F32)
    carry = (zero, zero, zero)
    for part, first, last in plan.chunks():
        cx = expansions(plan, cx_ref, part)

        def step(i, carry):
            rho, *edges = carry
            r = b_ref[pl.ds(i, n, stride=plan.rows), :] - spread(image_ref, cx, i)
            z = r / row_of(coef_ref, 0, i)
            at = pl.ds(pl.multiple_of(i * n, n), n)
            r_ref[at, :] = r
            z_ref[at, :] = z
            return (rho + r * z, *pack_edges(edges, z, i, z.shape[1]))

        carry = over_rows(first, last, step, carry)
    rho_ref[0] = carry[0]
    edge_ref[0] = z_ref[(plan.rows - 1) * n :, :]
    edge_ref[1] = z_ref[:n, :]
    edge_ref[2] = carry[2]
    edge_ref[3] = carry[1]


def image_kernel(plan, z_ref, edge_ref, coef_ref, mask_ref, hot_ref, dots_ref, f_ref, out_ref, s_ref):
    n = plan.loads
    cols = z_ref.shape[-1]
    zero = jnp.zeros((n, cols), F32)
    lane = lax.broadcasted_iota(jnp.int32, (n, cols), 1)
    s_ref[...] = jnp.zeros_like(s_ref)
    left_pack, right_pack = edge_ref[2], edge_ref[3]

    def image(i, z, up, down):
        before = jnp.where(lane == 0, pltpu.roll(left_pack, lax.rem(cols - i, cols), 1), pltpu.roll(z, 1, 1))
        after = jnp.where(lane == cols - 1, pltpu.roll(right_pack, cols - 1 - i, 1), pltpu.roll(z, cols - 1, 1))
        return (
            row_of(coef_ref, 0, i) * z
            - row_of(coef_ref, 1, i) * after
            - row_of(coef_ref, 2, i) * before
            - row_of(coef_ref, 3, i) * down
            - row_of(coef_ref, 4, i) * up
        )

    def load(i):
        return z_ref[pl.ds(pl.multiple_of(i * n, n), n), :]

    def step(i, carry):
        return finish(i, load(i), load(i - 1), load(i + 1), carry)

    def finish(i, z, up, down, carry):
        f = image(i, z, up, down)
        f_ref[pl.ds(pl.multiple_of(i * n, n), n), :] = f
        zf, *acc = carry
        return (zf + z * f, *[x + row_of(mask_ref, k, i) * f for k, x in enumerate(acc)])

    zf = zero
    for part, first, last in plan.chunks():
        carry = (zf,) + (zero,) * 4
        low, high = first, last
        if first == 0:
            carry = finish(0, load(0), edge_ref[0], load(1), carry)
            low = 1
        if last == plan.rows:
            high = last - 1
        while (high - low) % 4:
            carry = step(low, carry)
            low += 1
        carry = over_rows(low, high, step, carry)
        if last == plan.rows:
            carry = finish(last - 1, load(last - 1), load(last - 2), edge_ref[1], carry)
        zf, *acc = carry
        add_sums(plan, s_ref, part, acc)
    out_ref[...] = pack(hot_ref, s_ref, [dots_ref[k] for k in range(dots_ref.shape[0])] + [zf])


def second_kernel(plan, r_ref, f_ref, image_ref, coef_ref, cx_ref, alpha_ref, r1_ref, z1_ref, q_ref, dots_ref, edge_ref):
    n = plan.loads
    zero = jnp.zeros((n, r_ref.shape[-1]), F32)
    carry = (zero,) * 4
    alpha = alpha_ref[...]
    for part, first, last in plan.chunks():
        cx = expansions(plan, cx_ref, part)

        def step(i, carry):
            rho, qz, *edges = carry
            at = pl.ds(pl.multiple_of(i * n, n), n)
            q = f_ref[at, :] - spread(image_ref, cx, i)
            r = r_ref[at, :] - alpha * q
            z = r / row_of(coef_ref, 0, i)
            q_ref[at, :] = q
            r1_ref[at, :] = r
            z1_ref[at, :] = z
            return (rho + r * z, qz + q * z, *pack_edges(edges, z, i, z.shape[1]))

        carry = over_rows(first, last, step, carry)
    dots_ref[0] = carry[0]
    dots_ref[1] = carry[1]
    edge_ref[0] = z1_ref[(plan.rows - 1) * n :, :]
    edge_ref[1] = z1_ref[:n, :]
    edge_ref[2] = carry[3]
    edge_ref[3] = carry[2]


def last_kernel(plan, z_ref, z1_ref, r1_ref, f1_ref, q_ref, mask_ref, image_ref, cs_ref, cx_ref, scal_ref, s_out, r_out):
    n = plan.loads
    mix, alpha, beta = scal_ref[0], scal_ref[1], scal_ref[2]
    for part, first, last in plan.chunks():
        cs = expansions(plan, cs_ref, part)
        cx = expansions(plan, cx_ref, part)

        def step(i, carry):
            at = pl.ds(pl.multiple_of(i * n, n), n)
            to = pl.ds(i, n, stride=plan.rows)
            s_out[to, :] = spread(mask_ref, cs, i) + mix * z_ref[at, :] + alpha * z1_ref[at, :]
            q1 = f1_ref[at, :] - spread(image_ref, cx, i) + beta * q_ref[at, :]
            r_out[to, :] = r1_ref[at, :] - alpha * q1
            return carry

        over_rows(first, last, step, 0, 2)


def body(load_currents, labels, bump_height, horizontal_class, vertical_class, pad_class, edge_table, pad_table):
    rows, cols = labels.shape
    loads = load_currents.shape[0]
    regions = REG * REG
    grid_rows = lax.axis_size("row") * rows
    grid_cols = lax.axis_size("col") * cols
    height, width = grid_rows // REG, grid_cols // REG
    plan = Plan(rows, loads, height)
    levels = plan.levels
    ri, ci = lax.axis_index("row"), lax.axis_index("col")
    smem = pl.BlockSpec(memory_space=pltpu.SMEM)
    links, ends = pl.pallas_call(
        functools.partial(links_kernel, plan),
        out_shape=(shape(2, rows, cols), shape(4, 8, cols)),
        in_specs=[VM] * 4 + [smem],
        out_specs=(VM, VM),
        compiler_params=PARAMS,
    )(horizontal_class, vertical_class, labels, bump_height, edge_table)
    ends = exchange(ends, 5)
    mask, image, coef = pl.pallas_call(
        functools.partial(masks_kernel, plan, width),
        out_shape=(shape(4, rows, cols), shape(4, rows, cols), shape(5, rows, cols)),
        in_specs=[VM] * 5 + [smem],
        out_specs=(VM,) * 3,
        compiler_params=PARAMS,
    )(links, ends, labels, bump_height, pad_class, pad_table)

    span = cols // width + 2
    lane_base = (lax.iota(jnp.int32, cols) + width // 2) // width
    hot = jnp.stack([(lane_base[None] + b == lax.iota(jnp.int32, 8)[:, None]).astype(F32) for b in (0, 1)])
    count = lax.axis_size("row") * lax.axis_size("col")
    here = lax.broadcasted_iota(jnp.int32, (regions, 4 * count * 8), 0)
    sent = lax.broadcasted_iota(jnp.int32, (regions, 4 * count * 8), 1)
    level, device, x = sent // (count * 8), sent // 8 % count, sent % 8
    at_row = device // lax.axis_size("col") * (rows // height) - 1 + level
    at_col = device % lax.axis_size("col") * (cols // width) - 1 + x
    place = ((here // REG == at_row) & (here % REG == at_col) & (x < span) & (level < levels)).astype(jnp.bfloat16)
    here = lax.broadcasted_iota(jnp.int32, (regions, 2 * levels * cols), 0)
    lane = lax.broadcasted_iota(jnp.int32, (regions, 2 * levels * cols), 1)
    which, lane = lane // cols, lane % cols
    at_row = ri * (rows // height) - 1 + which % levels
    at_col = ci * (cols // width) - 1 + (lane + width // 2) // width + which // levels
    expand = ((here // REG == at_row) & (here % REG == at_col)).astype(jnp.bfloat16)

    def call(kernel, outs, *args, scratch=()):
        return pl.pallas_call(
            functools.partial(kernel, plan),
            out_shape=outs,
            in_specs=[VM] * len(args),
            out_specs=jax.tree.map(lambda _: VM, outs),
            scratch_shapes=scratch,
            compiler_params=PARAMS,
        )(*args)

    s_shape = shape(2, levels * loads, cols)
    sums_scratch = [pltpu.VMEM((2, 4 * BLOCK, cols), F32)]
    field = shape(rows * loads, cols)
    message = shape(8, 4 * BLOCK)
    coarse_shape = shape(regions, 4 * BLOCK)

    def image_of(z, edges, dots, ident):
        landed = exchange(edges, ident)
        f, sums = call(image_kernel, (field, message), z, landed, coef, mask, hot, dots, scratch=sums_scratch)
        return f, gather(sums, ident + 1).reshape(count * 8, 4 * BLOCK)

    flat = load_currents.reshape(loads * rows, cols)
    first = call(sums_kernel, shape(2, 8, 4 * BLOCK), flat, mask, image, hot, scratch=sums_scratch * 2)
    first = gather(first, 0)
    inverse = call(matrix_kernel, shape(regions, regions), first[:, 1].reshape(count * 8, 4 * BLOCK), place)
    cx, c0 = call(solve_first, (s_shape, coarse_shape), first[:, 0].reshape(count * 8, 4 * BLOCK), place, inverse, expand)
    r0, z0, rho_lanes, edges = call(
        first_kernel, (field, field, shape(1, loads, cols), shape(4, loads, cols)), flat, image, coef, cx
    )
    f0, sums = image_of(z0, edges, rho_lanes, 1)
    cx, c1, scal, alpha = call(
        solve_second, (s_shape, coarse_shape, shape(8, 4 * BLOCK), shape(loads, cols)), sums, place, inverse, expand
    )
    r1, z1, q0, dots, edges = call(
        second_kernel,
        (field, field, field, shape(2, loads, cols), shape(4, loads, cols)),
        r0, f0, image, coef, cx, alpha,
    )
    f1, sums = image_of(z1, edges, dots, 3)
    cs, cx, scal = call(
        solve_third, (s_shape, s_shape, shape(3, loads, cols)), sums, place, inverse, expand, c0, c1, scal
    )
    s, r = call(
        last_kernel, (shape(loads * rows, cols),) * 2,
        z0, z1, r1, f1, q0, mask, image, cs, cx, scal,
    )
    return (s.reshape(load_currents.shape), r.reshape(load_currents.shape))


def solution(mesh):
    grid = P("row", "col")
    cube = P(None, "row", "col")
    return jax.shard_map(
        body,
        mesh=mesh,
        in_specs=(cube, grid, grid, grid, grid, grid, P(), P()),
        out_specs=(cube, cube),
        check_vma=False,
    )
```
